32 devices in a mesh: chan: 8 (over z, x), row: 4 (over y, core).
Axes of the slice: x: 2, y: 2, z: 4, core: 2. Of those that a mesh axis runs over, the one named last changes fastest.
Arguments:
- generator: float32 [8, 2048, 2048], P('chan', 'row'), may hold values from -0.125 to 0.125
- hamiltonian: float32 [8, 2048, 2048], P('chan', 'row'), may hold values from -6 to 6
- pp_width: int32 [8], P('chan'), may hold values from 1025 to 2048
- pp_orbit: int32 [8, 2, 2048], P('chan'), may hold values from 0 to 239
- ph_width: int32 [32], P(('chan', 'row')), may hold values from 513 to 1024
- ph_orbit: int32 [32, 2, 1024], P(('chan', 'row')), may hold values from 0 to 239
- occupation: int32 [240], replicated, may hold values 0 or 1
- send_tile: int32 [32, 32, 4], P(('chan', 'row')), may hold values from 0 to 63, as said below
- ph_source: int32 [32, 64, 2], P(('chan', 'row')), may hold values from 0 to 127, as said below
- ph_coef: float32 [32, 64, 2], P(('chan', 'row')), may hold values from -1.5 to 1.5
Outputs:
- commutator: float32 [8, 2048, 2048], P('chan', 'row')
The draws below stay inside these ranges and needn't reach their ends.
Inputs may be any that keep to these rules, and one draw needn't show every extreme that they name: `send_tile`: every entry is a source tile number of device s; every slot carries a tile. ph_source[d] names every slot s * 4 + e exactly once.
All inputs are finite; a program needn't handle non-finite values.
Results may differ from the reference program's by a relative error of at most 0.0049.
Values may be sent and summed in bfloat16 or wider, within the bound.
A program may use at most 128 MiB of HBM per device.

```python
import jax
import jax.numpy as jnp
from jax import lax

W = 2048
PW = 1024
ORBITS = 240
TILE = 128
TERMS = 2
PEERS = 32
SLAB = 512
COL_TILES = 16
SRC_TILES = 64
PH_SIDE = 8
PH_TILES = 64
REFS = 128
CAP = 4
N_CHAN = 8
N_ROW = 4


def shuffle_peers(subkey):
    return jax.random.permutation(subkey, PEERS)


def shuffle_row(subkey, values):
    return jax.random.permutation(subkey, values)


def pandya_plan(key):
    used = REFS // CAP
    owner_keys = jax.random.split(jax.random.fold_in(key, 101), PEERS)
    orders = jax.vmap(shuffle_peers)(owner_keys)
    picks = jax.random.randint(jax.random.fold_in(key, 102), (PEERS, used, CAP), 0, SRC_TILES)
    position = jnp.argsort(orders, axis=1, stable=True)
    chosen = position < used
    lookup = jnp.broadcast_to(jnp.minimum(position, used - 1)[:, :, None], (PEERS, PEERS, CAP))
    gathered = jnp.take_along_axis(picks, lookup, axis=1)
    sending = jnp.where(chosen[:, :, None], gathered, -1).transpose(1, 0, 2)
    sources = orders[:, :used]
    flat_slots = (sources[:, :, None] * CAP + jnp.arange(CAP, dtype=jnp.int32)[None, None, :]).reshape(PEERS, REFS)
    mixing_keys = jax.random.split(jax.random.fold_in(key, 103), PEERS)
    mixed = jax.vmap(shuffle_row)(mixing_keys, flat_slots)
    return (sending.astype(jnp.int32), mixed.reshape(PEERS, PH_TILES, TERMS).astype(jnp.int32))


def draw_send_tile(key, part):
    return pandya_plan(key)[0]


def draw_ph_source(key, part):
    return pandya_plan(key)[1]


def set_ends(drawn, own_key, least, high):
    spot = [jax.random.randint(jax.random.fold_in(own_key, axis), (), 0, length) for axis, length in enumerate(drawn.shape)]
    main_axis = drawn.shape.index(max(drawn.shape))
    beside = spot[:main_axis] + [(spot[main_axis] + 1) % drawn.shape[main_axis]] + spot[main_axis + 1:]
    return drawn.at[tuple(spot)].set(least).at[tuple(beside)].set(high)


def steps_of(own_key, dims, cuts, low, top_value):
    loudness, own = 1.0, jax.random.fold_in(own_key, 6)
    for axis_at, shards_of in cuts:
        draws = jnp.exp(jax.random.uniform(jax.random.fold_in(own, axis_at), (shards_of,), jnp.float32, low / len(cuts), top_value / len(cuts)))
        loudness = loudness * jnp.repeat(draws, dims[axis_at] // shards_of).reshape([-1 if axis == axis_at else 1 for axis in range(len(dims))])
    return loudness


def normal_values(rng, extent, width, reach, cuts=(), kind=jnp.bfloat16):
    drawn = width * jax.random.normal(rng, extent, jnp.float32)
    if cuts:
        drawn = drawn * steps_of(rng, extent, cuts, -0.22, 0.18)
    return jnp.clip(drawn, -reach, reach).astype(kind)


def setup_inputs(seed: int = 0) -> dict:
    key_list = jax.random.split(jax.random.key(seed), 11)
    return {
        "generator": normal_values(key_list[0], (N_CHAN, W, W), W ** -0.5, 0.125, ((0, 8), (1, 4)), jnp.float32),
        "hamiltonian": normal_values(key_list[1], (N_CHAN, W, W), 1.0, 6.0, ((0, 8), (1, 4)), jnp.float32),
        "pp_width": set_ends(jax.random.randint(key_list[2], (N_CHAN,), W // 2 + 1, W + 1), jax.random.fold_in(key_list[2], 1), W // 2 + 1, W).astype(jnp.int32),
        "pp_orbit": set_ends(jax.random.randint(key_list[3], (N_CHAN, 2, W), 0, ORBITS), jax.random.fold_in(key_list[3], 1), 0, ORBITS - 1).astype(jnp.int32),
        "ph_width": set_ends(jax.random.randint(key_list[4], (PEERS,), PW // 2 + 1, PW + 1), jax.random.fold_in(key_list[4], 1), PW // 2 + 1, PW).astype(jnp.int32),
        "ph_orbit": set_ends(jax.random.randint(key_list[5], (PEERS, 2, PW), 0, ORBITS), jax.random.fold_in(key_list[5], 1), 0, ORBITS - 1).astype(jnp.int32),
        "occupation": set_ends((jax.random.randint(key_list[6], (ORBITS,), 0, 3) < 1).astype(jnp.int32), jax.random.fold_in(key_list[6], 1), 0, 1),
        "send_tile": draw_send_tile(jax.random.fold_in(key_list[10], 71), 0),
        "ph_source": draw_ph_source(jax.random.fold_in(key_list[10], 71), 0),
        "ph_coef": jnp.clip(jax.random.uniform(key_list[9], (PEERS, PH_TILES, TERMS), jnp.float32, -1.5, 1.5) * steps_of(key_list[9], (PEERS, PH_TILES, TERMS), ((0, 32),), -0.4, 0.0), -1.5, 1.5),
    }


def reference(generator, hamiltonian, pp_width, pp_orbit, ph_width, ph_orbit, occupation, send_tile, ph_source, ph_coef):
    occupied = occupation.astype(jnp.float32)
    columns = jnp.arange(W, dtype=jnp.int32)
    col_ok = columns[None, :] < pp_width[:, None]
    inside = col_ok[:, :, None] & col_ok[:, None, :]
    gen_b = jnp.where(inside, generator, 0.0).astype(jnp.bfloat16)
    ham_b = jnp.where(inside, hamiltonian, 0.0).astype(jnp.bfloat16)
    weight_pp = jnp.where(col_ok, 1.0 - occupied[pp_orbit[:, 0]] - occupied[pp_orbit[:, 1]], 0.0).astype(jnp.bfloat16)

    def direct_block(operands):
        gen_one, ham_one, factor = operands
        first = jnp.dot(gen_one * factor[None, :], ham_one, preferred_element_type=jnp.float32)
        second = jnp.dot(ham_one * factor[None, :], gen_one, preferred_element_type=jnp.float32)
        return first - second

    direct = lax.map(direct_block, (gen_b, ham_b, weight_pp))

    def split_tiles(blocks):
        shaped = blocks.reshape(N_CHAN, N_ROW, SLAB // TILE, TILE, COL_TILES, TILE)
        return shaped.transpose(0, 1, 2, 4, 3, 5).reshape(PEERS, SRC_TILES, TILE, TILE)

    gen_tiles = split_tiles(gen_b)
    ham_tiles = split_tiles(ham_b)
    hole_cols = jnp.arange(PW, dtype=jnp.int32)[None, :] < ph_width[:, None]
    weight_ph = jnp.where(hole_cols, occupied[ph_orbit[:, 0]] - occupied[ph_orbit[:, 1]], 0.0).astype(jnp.bfloat16)
    peer_ids = jnp.arange(PEERS, dtype=jnp.int32)

    def per_owner(collected, owner):
        references = ph_source[owner]
        coefficients = ph_coef[owner]
        sources = references // CAP
        slot_index = references % CAP
        tile_ids = send_tile[sources, owner, slot_index]

        def assemble(tiles):
            picked = tiles[sources, tile_ids].astype(jnp.float32)
            summed = jnp.sum(coefficients[:, :, None, None] * picked, axis=1).astype(jnp.bfloat16)
            return summed.reshape(PH_SIDE, PH_SIDE, TILE, TILE).transpose(0, 2, 1, 3).reshape(PW, PW)

        ph_gen = assemble(gen_tiles)
        ph_ham = assemble(ham_tiles)
        factor = weight_ph[owner]
        valid = hole_cols[owner]
        product = jnp.dot(ph_gen * factor[None, :], ph_ham, preferred_element_type=jnp.float32)
        product = product - jnp.dot(ph_ham * factor[None, :], ph_gen, preferred_element_type=jnp.float32)
        product = jnp.where(valid[:, None] & valid[None, :], product, 0.0).astype(jnp.bfloat16)
        comm_tiles = product.reshape(PH_SIDE, TILE, PH_SIDE, TILE).transpose(0, 2, 1, 3).reshape(PH_TILES, TILE, TILE).astype(jnp.float32)
        weighted = coefficients[:, :, None, None] * comm_tiles[:, None]
        returned = jnp.zeros((PEERS * CAP, TILE, TILE), jnp.float32).at[references.reshape(-1)].add(weighted.reshape(-1, TILE, TILE))
        returned = lax.optimization_barrier(returned.astype(jnp.bfloat16)).astype(jnp.float32)
        own_tiles = send_tile[:, owner, :]
        target = jnp.where(own_tiles >= 0, peer_ids[:, None] * SRC_TILES + own_tiles, PEERS * SRC_TILES).reshape(-1)
        return collected.at[target].add(returned), None

    start_pile = jnp.zeros((PEERS * SRC_TILES + 1, TILE, TILE), jnp.float32)
    collected, _ = lax.scan(per_owner, start_pile, peer_ids)
    back = collected[:-1].reshape(N_CHAN, N_ROW, SLAB // TILE, COL_TILES, TILE, TILE)
    back = back.transpose(0, 1, 2, 4, 3, 5).reshape(N_CHAN, W, W)
    return jnp.where(inside, direct + back, 0.0)
```

```python
import functools

import jax
import jax.numpy as jnp
from jax import lax
from jax.experimental import pallas as pl
from jax.experimental.pallas import tpu as pltpu
from jax.sharding import PartitionSpec as P

TILE = 128
F32 = jnp.float32
BF16 = jnp.bfloat16


def params(limit=60 << 20):
    return pltpu.CompilerParams(vmem_limit_bytes=limit)


def cost(moved, flops=0):
    return pl.CostEstimate(flops=flops, bytes_accessed=moved, transcendentals=0)


def select_kernel(row_tiles, step_slots, cap, idx, width, rows_left, x_ref, b_ref, out_ref, tiles):
    i = pl.program_id(0)

    @pl.when(i < row_tiles)
    def _():
        x = x_ref[...]
        rows = i * TILE + lax.broadcasted_iota(jnp.int32, x.shape, 0)
        cols = lax.broadcasted_iota(jnp.int32, x.shape, 1)
        v = jnp.where((rows < rows_left[0]) & (cols < width[0]), x, 0.0).astype(BF16)
        b_ref[...] = v
        col_tiles = x.shape[1] // TILE
        for c in range(col_tiles):
            tiles[i * col_tiles + c] = v[:, c * TILE : (c + 1) * TILE]

    @pl.when(i >= row_tiles)
    def _():
        first = (i - row_tiles) * step_slots
        for k in range(step_slots):
            s = first + k
            out_ref[k] = tiles[idx[s // cap, s % cap]]


def select_tiles(slab, width, rows_left, slots):
    rows, cols = slab.shape
    peers, cap = slots.shape
    total = peers * cap
    row_tiles = rows // TILE
    step_slots = 32
    return pl.pallas_call(
        functools.partial(select_kernel, row_tiles, step_slots, cap),
        grid_spec=pltpu.PrefetchScalarGridSpec(
            num_scalar_prefetch=3,
            grid=(row_tiles + total // step_slots,),
            in_specs=[pl.BlockSpec((TILE, cols), lambda i, *_: (jnp.minimum(i, row_tiles - 1), 0))],
            out_specs=(
                pl.BlockSpec((TILE, cols), lambda i, *_: (jnp.minimum(i, row_tiles - 1), 0)),
                pl.BlockSpec((step_slots, TILE, TILE), lambda i, *_: (jnp.maximum(i - row_tiles, 0), 0, 0)),
            ),
            scratch_shapes=[pltpu.VMEM((row_tiles * (cols // TILE), TILE, TILE), BF16)],
        ),
        out_shape=(
            jax.ShapeDtypeStruct((rows, cols), BF16),
            jax.ShapeDtypeStruct((total, TILE, TILE), BF16),
        ),
        compiler_params=params(),
        cost_estimate=cost(6 * rows * cols + 2 * total * TILE * TILE),
        name="select_tiles",
    )(slots, width, rows_left, slab)


def assemble_rows(i, side, src, coef, recv, dst, dst_w, w):
    for c in range(side):
        t = i * side + c
        one = recv[src[t, 0]].astype(F32) * coef[t, 0]
        two = recv[src[t, 1]].astype(F32) * coef[t, 1]
        tile = (one + two).astype(BF16)
        cols = slice(c * TILE, (c + 1) * TILE)
        rows = pl.ds(pl.multiple_of(i * TILE, TILE), TILE)
        dst[rows, cols] = tile
        dst_w[rows, cols] = tile * w[:, cols]


def assemble_kernel(side, src, coef, recv, w, g_ref, gw_ref):
    @pl.loop(0, side)
    def _(i):
        assemble_rows(i, side, src, coef, recv, g_ref, gw_ref, w)


def assemble(recv, src, coef, w):
    width = w.shape[1]
    smem = pl.BlockSpec(memory_space=pltpu.SMEM)
    vmem = pl.BlockSpec(memory_space=pltpu.VMEM)
    return pl.pallas_call(
        functools.partial(assemble_kernel, width // TILE),
        in_specs=[smem, smem, vmem, vmem],
        out_specs=(vmem, vmem),
        out_shape=(jax.ShapeDtypeStruct((width, width), BF16),) * 2,
        compiler_params=params(),
        cost_estimate=cost(2 * recv.size + 4 * width * width),
        name="assemble",
    )(src, coef, recv, w)


def commutator_kernel(side, src, coef, width, recv, w, g_ref, gw_ref, out_ref, h, hw, comm):
    @pl.loop(0, side)
    def _(i):
        assemble_rows(i, side, src, coef, recv, h, hw, w)

    full = side * TILE
    step = 2 * TILE

    @pl.loop(0, full // step)
    def _(j):
        cols = pl.ds(pl.multiple_of(j * step, step), step)
        c = jnp.dot(gw_ref[...], h[:, cols], preferred_element_type=F32)
        c = c - jnp.dot(hw[...], g_ref[:, cols], preferred_element_type=F32)
        row = lax.broadcasted_iota(jnp.int32, (full, step), 0)
        col = j * step + lax.broadcasted_iota(jnp.int32, (full, step), 1)
        comm[:, cols] = jnp.where((row < width[0]) & (col < width[0]), c, 0.0).astype(BF16)

    @pl.loop(0, side)
    def _(i):
        rows = pl.ds(pl.multiple_of(i * TILE, TILE), TILE)
        for c in range(side):
            t = i * side + c
            tile = comm[rows, c * TILE : (c + 1) * TILE].astype(F32)
            out_ref[src[t, 0]] = (tile * coef[t, 0]).astype(BF16)
            out_ref[src[t, 1]] = (tile * coef[t, 1]).astype(BF16)


def commutator(recv, src, coef, hole, w, g, gw):
    full = w.shape[1]
    smem = pl.BlockSpec(memory_space=pltpu.SMEM)
    vmem = pl.BlockSpec(memory_space=pltpu.VMEM)
    return pl.pallas_call(
        functools.partial(commutator_kernel, full // TILE),
        in_specs=[smem, smem, smem, vmem, vmem, vmem, vmem],
        out_specs=vmem,
        out_shape=jax.ShapeDtypeStruct(recv.shape, BF16),
        scratch_shapes=[pltpu.VMEM((full, full), BF16)] * 3,
        compiler_params=params(),
        cost_estimate=cost(4 * recv.size + 4 * full * full, 4 * full * full * full),
        name="commutator",
    )(src, coef, hole, recv, w, g, gw)


def finish_kernel(steps, step_slots, cap, col_tiles, idx, width, rows_left, arrived, direct, out_ref, acc):
    i = pl.program_id(0)

    @pl.when(i == 0)
    def _():
        acc[...] = direct[...]

    @pl.when(i < steps)
    def _():
        for k in range(step_slots):
            s = i * step_slots + k
            j = idx[s // cap, s % cap]
            rows = pl.ds(pl.multiple_of(j // col_tiles * TILE, TILE), TILE)
            cols = pl.ds(pl.multiple_of(j % col_tiles * TILE, TILE), TILE)
            acc[rows, cols] += arrived[k].astype(F32)

    @pl.when(i >= steps)
    def _():
        base = (i - steps) * TILE
        v = acc[pl.ds(pl.multiple_of(base, TILE), TILE), :]
        rows = base + lax.broadcasted_iota(jnp.int32, v.shape, 0)
        cols = lax.broadcasted_iota(jnp.int32, v.shape, 1)
        out_ref[...] = jnp.where((rows < rows_left[0]) & (cols < width[0]), v, 0.0)


def finish(arrived, direct, width, rows_left, slots):
    rows, cols = direct.shape
    peers, cap = slots.shape
    step_slots = 16
    steps = peers * cap // step_slots
    return pl.pallas_call(
        functools.partial(finish_kernel, steps, step_slots, cap, cols // TILE),
        grid_spec=pltpu.PrefetchScalarGridSpec(
            num_scalar_prefetch=3,
            grid=(steps + rows // TILE,),
            in_specs=[
                pl.BlockSpec((step_slots, TILE, TILE), lambda i, *_: (jnp.minimum(i, steps - 1), 0, 0)),
                pl.BlockSpec((rows, cols), lambda i, *_: (0, 0)),
            ],
            out_specs=pl.BlockSpec((TILE, cols), lambda i, *_: (jnp.maximum(i - steps, 0), 0)),
            scratch_shapes=[pltpu.VMEM((rows, cols), F32)],
        ),
        out_shape=jax.ShapeDtypeStruct((rows, cols), F32),
        compiler_params=params(),
        cost_estimate=cost(2 * arrived.size + 8 * rows * cols),
        name="finish",
    )(slots, width, rows_left, arrived, direct)


def occupancy(orbits, occupation):
    labels = jnp.arange(occupation.shape[0], dtype=jnp.int32)
    hit = (orbits[:, :, None] == labels) & (occupation == 1)
    return jnp.sum(hit.astype(F32), axis=2)


def exchange(tiles, peers):
    shaped = tiles.reshape((peers, -1) + tiles.shape[1:])
    moved = lax.all_to_all(shaped, ("chan", "row"), split_axis=0, concat_axis=0, tiled=True)
    return moved.reshape(tiles.shape)


def on_device(
    generator, hamiltonian, pp_width, pp_orbit, ph_width, ph_orbit, occupation, send_tile, ph_source, ph_coef
):
    slab_rows = generator.shape[1]
    full_width = generator.shape[2]
    hole_width = ph_orbit.shape[2]
    slots = send_tile[0]
    src = ph_source[0]
    coef = ph_coef[0]
    peers = slots.shape[0]
    rows_left = pp_width - lax.axis_index("row") * slab_rows

    gen_b, gen_out = select_tiles(generator[0], pp_width, rows_left, slots)
    got_gen = exchange(gen_out, peers)
    ham_in, gen_b = lax.optimization_barrier((hamiltonian[0], gen_b))
    ham_b, ham_out = select_tiles(ham_in, pp_width, rows_left, slots)
    got_ham = exchange(ham_out, peers)

    pp_orbit, ph_orbit, ham_b = lax.optimization_barrier((pp_orbit, ph_orbit, ham_b))
    col_ok = jnp.arange(full_width, dtype=jnp.int32) < pp_width[0]
    pair = occupancy(pp_orbit[0], occupation)
    weight_pp = jnp.where(col_ok, 1.0 - pair[0] - pair[1], 0.0).astype(BF16)
    hole_cols = jnp.arange(hole_width, dtype=jnp.int32) < ph_width[0]
    hole = occupancy(ph_orbit[0], occupation)
    weight_ph = jnp.where(hole_cols, hole[0] - hole[1], 0.0).astype(BF16)[None]

    gen_all = lax.all_gather(gen_b, "row", axis=0, tiled=True)
    ham_all = lax.all_gather(ham_b, "row", axis=0, tiled=True)
    first = jnp.dot(gen_b * weight_pp[None, :], ham_all, preferred_element_type=F32)
    second = jnp.dot(ham_b * weight_pp[None, :], gen_all, preferred_element_type=F32)
    direct = first - second

    ph_gen, ph_gen_w = assemble(got_gen, src, coef, weight_ph)
    returned = commutator(got_ham, src, coef, ph_width, weight_ph, ph_gen, ph_gen_w)
    arrived = exchange(returned, peers)
    return finish(arrived, direct, pp_width, rows_left, slots)[None]


def solution(mesh):
    in_specs = (
        P("chan", "row", None),
        P("chan", "row", None),
        P("chan"),
        P("chan", None, None),
        P(("chan", "row")),
        P(("chan", "row"), None, None),
        P(),
        P(("chan", "row"), None, None),
        P(("chan", "row"), None, None),
        P(("chan", "row"), None, None),
    )
    out_specs = P("chan", "row", None)
    return jax.shard_map(
        on_device, mesh=mesh, in_specs=in_specs, out_specs=out_specs, check_vma=False
    )
```

```python
import functools

import jax
import jax.numpy as jnp
from jax import lax
from jax.experimental import pallas as pl
from jax.experimental.pallas import tpu as pltpu
from jax.sharding import PartitionSpec as P

TILE = 128
F32 = jnp.float32
BF16 = jnp.bfloat16


def params(limit=60 << 20):
    return pltpu.CompilerParams(vmem_limit_bytes=limit)


def cost(moved, flops=0):
    return pl.CostEstimate(flops=flops, bytes_accessed=moved, transcendentals=0)


def select_kernel(
    row_tiles, steps, step_slots, cap, idx, width, rows_left, gen, ham, gen_b, ham_b, gen_out, ham_out, gen_tiles, ham_tiles
):
    i = pl.program_id(0)

    def cast(at, x_ref, b_ref, tiles):
        x = x_ref[...]
        rows = at * TILE + lax.broadcasted_iota(jnp.int32, x.shape, 0)
        cols = lax.broadcasted_iota(jnp.int32, x.shape, 1)
        v = jnp.where((rows < rows_left[0]) & (cols < width[0]), x, 0.0).astype(BF16)
        b_ref[...] = v
        col_tiles = x.shape[1] // TILE
        for c in range(col_tiles):
            tiles[at * col_tiles + c] = v[:, c * TILE : (c + 1) * TILE]

    def pick(at, out_ref, tiles):
        for k in range(step_slots):
            s = at * step_slots + k
            out_ref[k] = tiles[idx[s % cap, s // cap]]

    @pl.when(i < row_tiles)
    def _():
        cast(i, gen, gen_b, gen_tiles)

    @pl.when((i >= row_tiles) & (i < 2 * row_tiles))
    def _():
        cast(i - row_tiles, ham, ham_b, ham_tiles)

    @pl.when((i >= row_tiles) & (i < row_tiles + steps))
    def _():
        pick(i - row_tiles, gen_out, gen_tiles)

    @pl.when(i >= 2 * row_tiles)
    def _():
        pick(jnp.minimum(i - 2 * row_tiles, steps - 1), ham_out, ham_tiles)


def select_tiles(gen, ham, width, rows_left, slots):
    rows, cols = gen.shape
    cap, peers = slots.shape
    total = peers * cap
    row_tiles = rows // TILE
    steps = row_tiles
    step_slots = total // steps
    tiles = pltpu.VMEM((row_tiles * (cols // TILE), TILE, TILE), BF16)

    def window(first, count):
        return lambda i: jnp.clip(i - first, 0, count - 1)

    early, late = window(0, row_tiles), window(row_tiles, row_tiles)
    out_early, out_late = window(row_tiles, steps), window(2 * row_tiles, steps)
    slab = (TILE, cols)
    chunk = (step_slots, TILE, TILE)
    return pl.pallas_call(
        functools.partial(select_kernel, row_tiles, steps, step_slots, cap),
        grid_spec=pltpu.PrefetchScalarGridSpec(
            num_scalar_prefetch=3,
            grid=(2 * row_tiles + steps,),
            in_specs=[
                pl.BlockSpec(slab, lambda i, *_: (early(i), 0)),
                pl.BlockSpec(slab, lambda i, *_: (late(i), 0)),
            ],
            out_specs=(
                pl.BlockSpec(slab, lambda i, *_: (early(i), 0)),
                pl.BlockSpec(slab, lambda i, *_: (late(i), 0)),
                pl.BlockSpec(chunk, lambda i, *_: (out_early(i), 0, 0)),
                pl.BlockSpec(chunk, lambda i, *_: (out_late(i), 0, 0)),
            ),
            scratch_shapes=[tiles, tiles],
        ),
        out_shape=(jax.ShapeDtypeStruct((rows, cols), BF16),) * 2
        + (jax.ShapeDtypeStruct((total, TILE, TILE), BF16),) * 2,
        compiler_params=params(),
        cost_estimate=cost(12 * rows * cols + 4 * total * TILE * TILE),
        name="select_tiles",
    )(slots, width, rows_left, gen, ham)


def assemble_rows(i, side, src, coef, recv, dst, dst_w, w):
    for c in range(side):
        t = i * side + c
        one = recv[src[0, t]].astype(F32) * coef[0, t]
        two = recv[src[1, t]].astype(F32) * coef[1, t]
        tile = (one + two).astype(BF16)
        cols = slice(c * TILE, (c + 1) * TILE)
        rows = pl.ds(pl.multiple_of(i * TILE, TILE), TILE)
        dst[rows, cols] = tile
        dst_w[rows, cols] = tile * w[:, cols]


def commutator_kernel(side, src, coef, width, recv_gen, recv_ham, w, out_ref, ham_in, g, gw, h, hw, comm, sem):
    load = pltpu.make_async_copy(recv_ham, ham_in, sem)
    load.start()

    @pl.loop(0, side)
    def _(i):
        assemble_rows(i, side, src, coef, recv_gen, g, gw, w)

    load.wait()

    @pl.loop(0, side)
    def _(i):
        assemble_rows(i, side, src, coef, ham_in, h, hw, w)

    full = side * TILE
    step = 2 * TILE

    @pl.loop(0, full // step)
    def _(j):
        cols = pl.ds(pl.multiple_of(j * step, step), step)
        c = jnp.dot(gw[...], h[:, cols], preferred_element_type=F32)
        c = c - jnp.dot(hw[...], g[:, cols], preferred_element_type=F32)
        row = lax.broadcasted_iota(jnp.int32, (full, step), 0)
        col = j * step + lax.broadcasted_iota(jnp.int32, (full, step), 1)
        comm[:, cols] = jnp.where((row < width[0]) & (col < width[0]), c, 0.0).astype(BF16)

    @pl.loop(0, side)
    def _(i):
        rows = pl.ds(pl.multiple_of(i * TILE, TILE), TILE)
        for c in range(side):
            t = i * side + c
            tile = comm[rows, c * TILE : (c + 1) * TILE].astype(F32)
            out_ref[src[0, t]] = (tile * coef[0, t]).astype(BF16)
            out_ref[src[1, t]] = (tile * coef[1, t]).astype(BF16)


def commutator(recv_gen, recv_ham, src, coef, hole, w):
    full = w.shape[1]
    smem = pl.BlockSpec(memory_space=pltpu.SMEM)
    vmem = pl.BlockSpec(memory_space=pltpu.VMEM)
    return pl.pallas_call(
        functools.partial(commutator_kernel, full // TILE),
        in_specs=[smem, smem, smem, vmem, pl.BlockSpec(memory_space=pl.ANY), vmem],
        out_specs=vmem,
        out_shape=jax.ShapeDtypeStruct(recv_gen.shape, BF16),
        scratch_shapes=[pltpu.VMEM(recv_ham.shape, BF16)]
        + [pltpu.VMEM((full, full), BF16)] * 5
        + [pltpu.SemaphoreType.DMA],
        compiler_params=params(),
        cost_estimate=cost(6 * recv_gen.size, 4 * full * full * full),
        name="commutator",
    )(src, coef, hole, recv_gen, recv_ham, w)


def finish_kernel(steps, step_slots, cap, col_tiles, idx, width, rows_left, arrived, direct, out_ref, acc):
    i = pl.program_id(0)

    @pl.when(i == 0)
    def _():
        acc[...] = jnp.zeros_like(acc)

    @pl.when(i < steps)
    def _():
        for k in range(step_slots):
            s = i * step_slots + k
            j = idx[s % cap, s // cap]
            rows = pl.ds(pl.multiple_of(j // col_tiles * TILE, TILE), TILE)
            cols = pl.ds(pl.multiple_of(j % col_tiles * TILE, TILE), TILE)
            acc[rows, cols] += arrived[k].astype(F32)

    @pl.when(i >= steps)
    def _():
        base = (i - steps) * TILE
        v = acc[pl.ds(pl.multiple_of(base, TILE), TILE), :] + direct[...]
        rows = base + lax.broadcasted_iota(jnp.int32, v.shape, 0)
        cols = lax.broadcasted_iota(jnp.int32, v.shape, 1)
        out_ref[...] = jnp.where((rows < rows_left[0]) & (cols < width[0]), v, 0.0)


def finish(arrived, direct, width, rows_left, slots):
    rows, cols = direct.shape
    cap, peers = slots.shape
    step_slots = 16
    steps = peers * cap // step_slots
    return pl.pallas_call(
        functools.partial(finish_kernel, steps, step_slots, cap, cols // TILE),
        grid_spec=pltpu.PrefetchScalarGridSpec(
            num_scalar_prefetch=3,
            grid=(steps + rows // TILE,),
            in_specs=[
                pl.BlockSpec((step_slots, TILE, TILE), lambda i, *_: (jnp.minimum(i, steps - 1), 0, 0)),
                pl.BlockSpec((TILE, cols), lambda i, *_: (jnp.maximum(i - steps, 0), 0)),
            ],
            out_specs=pl.BlockSpec((TILE, cols), lambda i, *_: (jnp.maximum(i - steps, 0), 0)),
            scratch_shapes=[pltpu.VMEM((rows, cols), F32)],
        ),
        out_shape=jax.ShapeDtypeStruct((rows, cols), F32),
        compiler_params=params(),
        cost_estimate=cost(2 * arrived.size + 8 * rows * cols),
        name="finish",
    )(slots, width, rows_left, arrived, direct)


def occupancy(orbits, occupation):
    labels = jnp.arange(occupation.shape[0], dtype=jnp.int32)
    hit = (orbits[:, :, None] == labels) & (occupation == 1)
    return jnp.sum(hit.astype(F32), axis=2)


def forward_kernel(
    n_row, gen_in, ham_in, gen_b, ham_b, got_gen, got_ham, gen_rest, ham_rest, send, recv, ysend, yrecv, csend, crecv, local
):
    mesh_id = pl.DeviceIdType.MESH
    chan = lax.axis_index("chan")
    row = lax.axis_index("row")
    peers = gen_in.shape[0]
    me = chan * n_row + row
    group = peers // 4
    plane = me // group
    inner = lax.rem(me, group)
    n_y = n_row // 2
    y = row // 2
    core = lax.rem(row, 2)
    arrays = ((gen_in, got_gen), (ham_in, got_ham))
    slabs = ((gen_b, gen_rest), (ham_b, ham_rest))

    def place(p):
        return (p // n_row, lax.rem(p, n_row))

    barrier = pltpu.get_barrier_semaphore()

    @pl.loop(1, peers)
    def _(k):
        pl.semaphore_signal(barrier, inc=1, device_id=place(lax.rem(me + k, peers)), device_id_type=mesh_id)

    pl.semaphore_wait(barrier, peers - 1)

    def tile_copy(which, a, b):
        p = lax.rem(plane + a, 4) * group + lax.rem(inner + b, group)
        src, dst = arrays[which]
        k = a * group + b
        return pltpu.make_async_remote_copy(
            src_ref=src.at[p],
            dst_ref=dst.at[me],
            send_sem=send.at[which, k],
            recv_sem=recv.at[which, k],
            device_id=place(p),
            device_id_type=mesh_id,
        )

    def slab_copy(which, dy):
        src, dst = slabs[which]
        return pltpu.make_async_remote_copy(
            src_ref=src,
            dst_ref=dst.at[2 * dy - 1],
            send_sem=ysend.at[which, dy],
            recv_sem=yrecv.at[which, dy],
            device_id=(chan, lax.rem(y + dy, n_y) * 2 + core),
            device_id_type=mesh_id,
        )

    def core_copy(which, dy):
        src, dst = slabs[which]
        return pltpu.make_async_remote_copy(
            src_ref=src if dy == 0 else dst.at[2 * dy - 1],
            dst_ref=dst.at[2 * dy],
            send_sem=csend.at[which, dy],
            recv_sem=crecv.at[which, dy],
            device_id=(chan, y * 2 + 1 - core),
            device_id_type=mesh_id,
        )

    own = [pltpu.make_async_copy(arrays[w][0].at[me], arrays[w][1].at[me], local.at[w]) for w in range(2)]
    for w in range(2):
        own[w].start()
        core_copy(w, 0).start()
    turn = plane * plane // 4

    @pl.loop(0, 3)
    def _(i):
        a = 1 + lax.rem(i + turn, 3)

        @pl.loop(0, group)
        def _(b):
            tile_copy(0, a, b).start()
            tile_copy(1, a, b).start()

    for dy in range(1, n_y):
        for w in range(2):
            slab_copy(w, dy).start()

    @pl.loop(1, group)
    def _(b):
        tile_copy(0, 0, b).start()
        tile_copy(1, 0, b).start()

    for dy in range(1, n_y):
        for w in range(2):
            slab_copy(w, dy).wait()
            core_copy(w, dy).start()

    @pl.loop(1, peers)
    def _(k):
        for w in range(2):
            tile_copy(w, k // group, lax.rem(k, group)).wait()

    for w in range(2):
        own[w].wait()
        for dy in range(n_y):
            core_copy(w, dy).wait()


def forward(gen_out, ham_out, gen_b, ham_b, peers, n_row):
    shape = (peers, gen_out.shape[0] // peers) + gen_out.shape[1:]
    rest = (n_row - 1,) + gen_b.shape
    hbm = pl.BlockSpec(memory_space=pl.ANY)
    dma = pltpu.SemaphoreType.DMA
    got_gen, got_ham, gen_rest, ham_rest = pl.pallas_call(
        functools.partial(forward_kernel, n_row),
        in_specs=[hbm] * 4,
        out_specs=(hbm,) * 4,
        out_shape=(jax.ShapeDtypeStruct(shape, BF16),) * 2 + (jax.ShapeDtypeStruct(rest, BF16),) * 2,
        scratch_shapes=[
            dma((2, peers)),
            dma((2, peers)),
            dma((2, n_row)),
            dma((2, n_row)),
            dma((2, n_row)),
            dma((2, n_row)),
            dma((2,)),
        ],
        compiler_params=pltpu.CompilerParams(
            collective_id=0, has_side_effects=True, vmem_limit_bytes=60 << 20
        ),
        cost_estimate=cost(8 * gen_out.size),
        name="forward",
    )(gen_out.reshape(shape), ham_out.reshape(shape), gen_b, ham_b)
    return got_gen.reshape(gen_out.shape), got_ham.reshape(ham_out.shape), gen_rest, ham_rest


def ordered(left, order, rows):
    return jnp.concatenate([lax.dynamic_slice_in_dim(left, o * rows, rows, axis=1) for o in order], axis=1)


def exchange(tiles, peers):
    shaped = tiles.reshape((peers, -1) + tiles.shape[1:])
    moved = lax.all_to_all(shaped, ("chan", "row"), split_axis=0, concat_axis=0, tiled=True)
    return moved.reshape(tiles.shape)


def on_device(
    generator, hamiltonian, pp_width, pp_orbit, ph_width, ph_orbit, occupation, send_tile, ph_source, ph_coef
):
    slab_rows = generator.shape[1]
    full_width = generator.shape[2]
    hole_width = ph_orbit.shape[2]
    slots = send_tile[0].T
    src = ph_source[0].T
    coef = ph_coef[0].T
    peers = slots.shape[1]
    rows_left = pp_width - lax.axis_index("row") * slab_rows

    gen_b, ham_b, gen_out, ham_out = select_tiles(generator[0], hamiltonian[0], pp_width, rows_left, slots)
    n_row = full_width // slab_rows
    got_gen, got_ham, gen_rest, ham_rest = forward(gen_out, ham_out, gen_b, ham_b, peers, n_row)

    col_ok = jnp.arange(full_width, dtype=jnp.int32) < pp_width[0]
    pair = occupancy(pp_orbit[0], occupation)
    weight_pp = jnp.where(col_ok, 1.0 - pair[0] - pair[1], 0.0).astype(BF16)
    hole_cols = jnp.arange(hole_width, dtype=jnp.int32) < ph_width[0]
    hole = occupancy(ph_orbit[0], occupation)
    weight_ph = jnp.where(hole_cols, hole[0] - hole[1], 0.0).astype(BF16)[None]

    row = lax.axis_index("row")
    y, core = row // 2, row % 2
    order = []
    for dy in range(n_row // 2):
        other = (y + n_row // 2 - dy) % (n_row // 2)
        order += [other * 2 + core, other * 2 + 1 - core]
    gen_all = jnp.concatenate([gen_b, gen_rest.reshape(-1, full_width)])
    ham_all = jnp.concatenate([ham_b, ham_rest.reshape(-1, full_width)])
    first = jnp.dot(ordered(gen_b * weight_pp[None, :], order, slab_rows), ham_all, preferred_element_type=F32)
    second = jnp.dot(ordered(ham_b * weight_pp[None, :], order, slab_rows), gen_all, preferred_element_type=F32)
    direct = first - second

    returned = commutator(got_gen, got_ham, src, coef, ph_width, weight_ph)
    arrived = exchange(returned, peers)
    return finish(arrived, direct, pp_width, rows_left, slots)[None]


def solution(mesh):
    in_specs = (
        P("chan", "row", None),
        P("chan", "row", None),
        P("chan"),
        P("chan", None, None),
        P(("chan", "row")),
        P(("chan", "row"), None, None),
        P(),
        P(("chan", "row"), None, None),
        P(("chan", "row"), None, None),
        P(("chan", "row"), None, None),
    )
    out_specs = P("chan", "row", None)
    return jax.shard_map(
        on_device, mesh=mesh, in_specs=in_specs, out_specs=out_specs, check_vma=False
    )
```
